512 devices in a mesh: sec: 16 (over z_lo, x), dev: 32 (over y, z_hi, core).
Axes of the slice: x: 4, y: 8, z: 8 (z_hi: 2, z_lo: 4; z = z_hi * 4 + z_lo), core: 2. Of those that a mesh axis runs over, the one named last changes fastest.
Arguments:
- tile_inverse: bfloat16 [512, 4, 512, 512], P(('sec', 'dev'))
- link_coupling: bfloat16 [512, 512, 2048], P(('sec', 'dev')), may hold values from -0.125 to 0.125
- link_panels: int32 [512, 4], P(('sec', 'dev')), may hold values from 0 to 63, all different within a row
- leaf_rhs: bfloat16 [512, 48, 2048], P(('sec', 'dev')), may hold values from -6 to 6
- leaf_scale: float32 [512, 2048], P(('sec', 'dev')), may hold values from 0.1 to 0.5
- link_scale: float32 [8192], replicated, may hold values from 0.2 to 2
- link_inverse: bfloat16 [8192, 8192], P('sec', 'dev'), as said below
Outputs:
- leaf_step: bfloat16 [512, 48, 2048], P(('sec', 'dev'))
- link_step: bfloat16 [48, 8192], P(None, 'dev')
The draws below stay inside these ranges and needn't reach their ends.
Inputs may be any that keep to these rules, and one draw needn't show every extreme that they name: `link_panels`: the 4 panels of one block are different. link_inverse is symmetric.
All inputs are finite; a program needn't handle non-finite values.
Results may differ from the reference program's by a relative error of at most 0.02.
Values may be sent and summed in bfloat16 or wider, within the bound.
No kernel may reach another device: no remote copies, remote signals or barrier semaphores. Data moves between devices by JAX's collectives and lax.ppermute only.
A program may use at most 64 MiB of HBM per device.

```python
import math
import jax
import jax.numpy as jnp
from jax import lax

NB = 2048
TILE = 512
LINK = 8192
PANEL = 128
PB = 4
COLS = 48
SOLVES = 5
BLOCKS = 512


def draw_tile_inverse(key, part):
    first_key, second_key = jax.random.split(jax.random.fold_in(key, 11))
    shape = (BLOCKS, NB // TILE, TILE, TILE)
    noise = jax.random.truncated_normal(first_key, -4.0, 4.0, shape, jnp.float32)
    diag_values = jnp.exp(jax.random.uniform(second_key, (BLOCKS, NB // TILE, TILE), jnp.float32, math.log(0.5), math.log(2.0)))
    tiles = noise * (0.5 / math.sqrt(TILE)) + diag_values[..., None] * jnp.eye(TILE, dtype=jnp.float32)
    return tiles.astype(jnp.bfloat16)


def draw_link_inverse(key, part):
    first_key, second_key = jax.random.split(jax.random.fold_in(key, 23))
    noise = jax.random.normal(first_key, (LINK, LINK), jnp.float32)
    diag_values = jnp.exp(jax.random.uniform(second_key, (LINK,), jnp.float32, math.log(0.1), math.log(0.3)))
    symmetric = (noise + noise.T) * (0.05 / math.sqrt(2.0 * LINK))
    return (symmetric + jnp.diag(diag_values)).astype(jnp.bfloat16)


def steps_of(stream_key, extent, pieces, low, top_value):
    def one(position, blocks):
        steps = jax.random.uniform(jax.random.fold_in(jax.random.fold_in(stream_key, 6), position), (blocks,), jnp.float32, low / len(pieces), top_value / len(pieces))
        return jnp.repeat(jnp.exp(steps), extent[position] // blocks).reshape((-1,) + (1,) * (len(extent) - position - 1))

    gain = one(*pieces[0])
    for cut in pieces[1:]:
        gain = gain * one(*cut)
    return gain


def different_ones(stream_key, rows, number_of, top, lift):
    order = jax.random.permutation(jax.random.fold_in(stream_key, 1), number_of)
    pull = order
    for power in range(3):
        pull = pull * pull // number_of
    pull = pull * lift // number_of
    chance = jax.random.randint(jax.random.fold_in(stream_key, 2), (rows, number_of), 0, 4096) + pull
    sure = jax.random.permutation(jax.random.fold_in(stream_key, 3), rows)[jnp.arange(number_of) % rows]
    chance = jnp.where(jnp.arange(rows)[:, None] == sure[None, :], 1 << 14, chance)
    score = chance * number_of + jnp.arange(number_of)
    return lax.top_k(score.astype(jnp.int32), top)[1].astype(jnp.int32)


def gaussian(key, shape, scale, limit, shards=(), held_as=jnp.bfloat16):
    gain = steps_of(key, shape, shards, -0.22, 0.18) if shards else 1.0
    values = jax.random.normal(key, shape, jnp.float32) * scale * gain
    return jnp.minimum(jnp.maximum(values, -limit), limit).astype(held_as)


def setup_inputs(seed: int = 0) -> dict:
    keys = jax.random.split(jax.random.key(seed), 8)
    return {
        "tile_inverse": draw_tile_inverse(jax.random.fold_in(keys[7], 71), 0),
        "link_coupling": gaussian(keys[1], (BLOCKS, PB * PANEL, NB), NB ** -0.5, 0.125, ((0, 512),)),
        "link_panels": different_ones(keys[2], BLOCKS, LINK // PANEL, PB, 0),
        "leaf_rhs": gaussian(keys[3], (BLOCKS, COLS, NB), 1.0, 6.0, ((0, 512),)),
        "leaf_scale": jnp.clip(jnp.exp(math.log(0.5) - 1.609438 * jax.random.uniform(keys[4], (BLOCKS, NB), jnp.float32) ** steps_of(keys[4], (BLOCKS, NB), ((0, 512),), -0.2, 0.2)), 0.1, 0.5),
        "link_scale": jnp.clip(jnp.exp(jax.random.uniform(keys[5], (LINK,), jnp.float32, math.log(0.2), math.log(2.0))), 0.2, 2.0),
        "link_inverse": draw_link_inverse(jax.random.fold_in(keys[7], 71), 0),
    }


def apply_tiles(tile_inv, vectors):
    columns = vectors.shape[0]
    blocked = vectors.astype(jnp.float32).reshape(columns, NB // TILE, TILE)
    result = jnp.einsum("tab,ctb->cta", tile_inv.astype(jnp.float32), blocked)
    return result.reshape(columns, NB)


def reference(tile_inverse, link_coupling, link_panels, leaf_rhs, leaf_scale, link_scale, link_inverse):
    panel_count = LINK // PANEL
    selectors = (link_panels[:, :, None] == jnp.arange(panel_count, dtype=jnp.int32)[None, None, :]).astype(jnp.float32)
    previous = jnp.zeros(leaf_rhs.shape, jnp.bfloat16)
    linking = jnp.zeros((COLS, LINK), jnp.bfloat16)
    for solve_index in range(SOLVES):
        corrected = (leaf_rhs.astype(jnp.float32) - leaf_scale[:, None, :] * previous.astype(jnp.float32)).astype(jnp.bfloat16)

        def forward(summed, block_items):
            tile_inv, coupling, selector, right_side = block_items
            solved = apply_tiles(tile_inv, right_side).astype(jnp.bfloat16)
            touched = jnp.dot(solved, coupling.T, preferred_element_type=jnp.float32)
            spread = jnp.einsum("csr,sq->cqr", touched.reshape(COLS, PB, PANEL), selector)
            spread = spread.reshape(COLS, LINK).astype(jnp.bfloat16)
            return summed + spread.astype(jnp.float32), None

        summed, ignored = lax.scan(forward, jnp.zeros((COLS, LINK), jnp.float32),
                                   (tile_inverse, link_coupling, selectors, corrected))
        link_side = -link_scale[None, :] * linking.astype(jnp.float32)
        link_rhs = (link_side - summed).astype(jnp.bfloat16)
        linking = jnp.dot(link_rhs, link_inverse, preferred_element_type=jnp.float32).astype(jnp.bfloat16)
        link_now = linking

        def backward(block_items):
            tile_inv, coupling, selector, right_side = block_items
            picked = jnp.einsum("cqr,sq->csr", link_now.astype(jnp.float32).reshape(COLS, panel_count, PANEL), selector)
            picked = picked.reshape(COLS, PB * PANEL).astype(jnp.bfloat16)
            pushed = jnp.dot(picked, coupling, preferred_element_type=jnp.float32)
            reduced = (right_side.astype(jnp.float32) - pushed).astype(jnp.bfloat16)
            return apply_tiles(tile_inv, reduced).astype(jnp.bfloat16)

        previous = lax.map(backward, (tile_inverse, link_coupling, selectors, corrected))
    return previous, linking
```

```python
import functools

import jax
import jax.numpy as jnp
from jax import lax
from jax.experimental import pallas as pl
from jax.experimental.pallas import tpu as pltpu
from jax.sharding import Mesh, PartitionSpec as P

PANEL = 128
PB = 4
SOLVES = 5
ROWS = 8
SPLIT = ("zlo", "x", "y", "zhi", "core")
Z = ("zhi", "zlo")
GROUP = ("x", "y", "core")
BF16 = jnp.bfloat16
F32 = jnp.float32


def member_of(panel):
    x = ((panel >> 2) & 1) * 2 + (panel & 1)
    return x * 16 + (panel >> 3) * 2 + ((panel >> 1) & 1)


def dot(a, b):
    return lax.dot_general(a, b, (((1,), (0,)), ((), ())), preferred_element_type=F32)


def dot_t(a, b):
    return lax.dot_general(a, b, (((1,), (1,)), ((), ())), preferred_element_type=F32)


def by_tiles(tile_ref, vectors):
    tiles, size = tile_ref.shape[0], tile_ref.shape[1]
    return jnp.concatenate(
        [dot_t(vectors[:, t * size : (t + 1) * size], tile_ref[t]) for t in range(tiles)], axis=1
    ).astype(BF16)


def send_touched(corrected, tile_ref, coupling_ref, pack_ref, out_ref):
    solved = by_tiles(tile_ref, corrected)
    touched = dot_t(solved, coupling_ref[...]).astype(BF16)
    rows = jnp.concatenate([touched[:, s * PANEL : (s + 1) * PANEL] for s in range(PB)], axis=0)
    out_ref[...] = dot(pack_ref[...], rows).astype(BF16)


def solve_leaf(pieces_ref, unpack_ref, corrected_ref, tile_ref, coupling_ref):
    columns = corrected_ref.shape[0]
    rows = dot(unpack_ref[...], pieces_ref[...]).astype(BF16)
    panels = [rows[s * columns : (s + 1) * columns] for s in range(rows.shape[0] // columns)]
    picked = jnp.concatenate(panels[:PB], axis=1)
    pushed = dot(picked, coupling_ref[...])
    reduced = (corrected_ref[...].astype(F32) - pushed).astype(BF16)
    return by_tiles(tile_ref, reduced), panels[PB:]


def first_kernel(rhs_ref, tile_ref, coupling_ref, pack_ref, out_ref):
    send_touched(rhs_ref[...], tile_ref, coupling_ref, pack_ref, out_ref)


def middle_kernel(
    pieces_ref, unpack_ref, pack_ref, corrected_ref, rhs_ref, scale_ref, tile_ref, coupling_ref,
    out_ref, next_ref,
):
    leaf, _ = solve_leaf(pieces_ref, unpack_ref, corrected_ref, tile_ref, coupling_ref)
    corrected = (rhs_ref[...].astype(F32) - scale_ref[...] * leaf.astype(F32)).astype(BF16)
    next_ref[...] = corrected
    send_touched(corrected, tile_ref, coupling_ref, pack_ref, out_ref)


def last_kernel(
    pieces_ref, unpack_ref, corrected_ref, tile_ref, coupling_ref, leaf_ref, link_ref
):
    leaf, link = solve_leaf(pieces_ref, unpack_ref, corrected_ref, tile_ref, coupling_ref)
    leaf_ref[...] = leaf
    link_ref[...] = jnp.concatenate(link, axis=1)


def select_kernel(select_ref, pieces_ref, out_ref):
    out_ref[...] = dot(select_ref[...], pieces_ref[...]).astype(BF16)


def rhs_kernel(pieces_ref, step_ref, scale_ref, out_ref):
    members = pieces_ref.shape[0]
    summed = pieces_ref[0].astype(F32)
    for m in range(1, members):
        summed = summed + pieces_ref[m].astype(F32)
    rhs = (-scale_ref[...] * step_ref[...].astype(F32) - summed).astype(BF16)
    for m in range(members):
        out_ref[m] = rhs


def step_kernel(order, pieces_ref, inverse_ref, out_ref, step_ref):
    rhs = jnp.concatenate([pieces_ref[m] for m in order], axis=1)
    step = dot(rhs, inverse_ref[...]).astype(BF16)
    step_ref[...] = step
    for m in range(out_ref.shape[0]):
        out_ref[m] = step


def call(body, name, shapes, *operands):
    single = not isinstance(shapes, list)
    space = pl.BlockSpec(memory_space=pltpu.VMEM)
    out = pl.pallas_call(
        body,
        name=name,
        out_shape=[jax.ShapeDtypeStruct(s, BF16) for s in ([shapes] if single else shapes)],
        in_specs=[space] * len(operands),
        out_specs=[space] * (1 if single else len(shapes)),
        compiler_params=pltpu.CompilerParams(vmem_limit_bytes=24 << 20),
        interpret=jax.default_backend() == "cpu" and INTERPRET,
    )(*operands)
    return out[0] if single else out


INTERPRET = False


def swap(x, axes):
    return lax.all_to_all(x, axes, 0, 0, tiled=True)


def per_device(
    tile_inverse, link_coupling, link_panels, leaf_rhs, leaf_scale, link_scale, link_inverse
):
    tile_inv, coupling, own_rhs, own_scale = tile_inverse[0], link_coupling[0], leaf_rhs[0], leaf_scale
    columns = own_rhs.shape[0]
    zs, members = lax.axis_size(Z), lax.axis_size(GROUP)
    per_set = columns // zs
    x, y, core = lax.axis_index("x"), lax.axis_index("y"), lax.axis_index("core")
    zhi = lax.axis_index("zhi")

    panel = y * 8 + (x >> 1) * 4 + core * 2 + (x & 1)
    quarter = link_inverse.shape[0] // 2
    halves = link_inverse.reshape(2, quarter, 2, PANEL).transpose(0, 2, 1, 3)
    sent = jnp.broadcast_to(halves[:, None], (2, 2, 2, quarter, PANEL)).reshape(8, quarter, PANEL)
    got = swap(sent, ("zhi", "x")).reshape(2, 4, quarter, PANEL)
    got = lax.dynamic_index_in_dim(got, x >> 1, 0, keepdims=False).reshape(1, 4 * quarter, PANEL)
    inverse = swap(jnp.broadcast_to(got, (zs, 4 * quarter, PANEL)), Z).reshape(-1, PANEL)
    order = [
        member_of(zl * 16 + xx * 4 + zh * 2 + rh)
        for zh in range(2) for zl in range(4) for xx in range(4) for rh in range(2)
    ]
    scale = lax.dynamic_slice_in_dim(link_scale, panel * PANEL, PANEL)[None]

    peer_panels = swap(jnp.broadcast_to(link_panels, (zs, PB)), Z)
    out_panels = (y * 8 + core * 2) + (jnp.arange(zs)[:, None] // 4) * 4 + jnp.arange(2)[None]
    wide = member_of(jnp.concatenate([peer_panels, out_panels.astype(jnp.int32)], axis=1))

    def selector(peers):
        hit = peers[:, :, None, None, None] == jnp.arange(members)[None, None, None, :, None]
        same = jnp.arange(ROWS)[:, None, None] == jnp.arange(ROWS)[None, None, :]
        return (hit & same[None, None]).astype(BF16).reshape(-1, members * ROWS)

    def unpacker(panels):
        zi, s, c = jnp.arange(zs), jnp.arange(panels), jnp.arange(ROWS)
        hit = (
            (s[:, None, None, None, None, None] == s[None, None, None, None, :, None])
            & (c[:per_set][None, :, None, None, None, None] == c[None, None, None, None, None, :])
            & (zi[None, None, :, None, None, None] == zi[None, None, None, :, None, None])
        )
        return hit.astype(BF16).reshape(panels * columns, zs * panels * ROWS)

    pick, pick_wide = selector(wide[:, :PB]), selector(wide)
    spread = pick.T
    unpack, unpack_wide = unpacker(PB), unpacker(PB + 2)
    pack = unpack.T

    home = (zs * PB * ROWS, PANEL)
    flat = (members * ROWS, PANEL)
    group = (members, ROWS, PANEL)
    corrected = own_rhs
    step = jnp.zeros((ROWS, PANEL), BF16)
    pieces = call(first_kernel, "first", home, own_rhs, tile_inv, coupling, pack)
    for solve_index in range(SOLVES):
        last = solve_index == SOLVES - 1
        pieces = swap(pieces.reshape(zs, PB * ROWS, PANEL), Z).reshape(home)
        pieces = call(select_kernel, "spread", flat, spread, pieces)
        pieces = swap(pieces.reshape(group), GROUP)
        pieces = swap(call(rhs_kernel, "rhs", group, pieces, step, scale), GROUP)
        pieces, step = call(
            functools.partial(step_kernel, order), "step", [group, (ROWS, PANEL)], pieces, inverse
        )
        pieces = swap(pieces, GROUP).reshape(flat)
        picker = pick_wide if last else pick
        pieces = call(select_kernel, "pick", (picker.shape[0], PANEL), picker, pieces)
        pieces = swap(pieces.reshape(zs, -1, PANEL), Z).reshape(-1, PANEL)
        if last:
            leaf, link = call(
                last_kernel, "last", [own_rhs.shape, (columns, 2 * PANEL)],
                pieces, unpack_wide, corrected, tile_inv, coupling,
            )
        else:
            pieces, corrected = call(
                middle_kernel, "middle", [home, own_rhs.shape],
                pieces, unpack, pack, corrected, own_rhs, own_scale, tile_inv, coupling,
            )
    return leaf[None], link


def solution(mesh):
    fine = Mesh(mesh.devices.reshape(4, 4, 8, 2, 2), SPLIT)
    sec, dev = SPLIT[:2], SPLIT[2:]
    in_specs = (
        P(SPLIT, None, None, None),
        P(SPLIT, None, None),
        P(SPLIT, None),
        P(SPLIT, None, None),
        P(SPLIT, None),
        P(),
        P(sec, dev),
    )
    out_specs = (P(SPLIT, None, None), P(None, dev))
    return jax.shard_map(
        per_device, mesh=fine, in_specs=in_specs, out_specs=out_specs, check_vma=False
    )
```

```python
import jax
import jax.numpy as jnp
from jax import lax
from jax.experimental import pallas as pl
from jax.experimental.pallas import tpu as pltpu
from jax.sharding import Mesh, PartitionSpec as P

PANEL = 128
PB = 4
SOLVES = 5
ROWS = 8
SETS = 8
PER_SET = 6
SPLIT = ("zlo", "x", "y", "zhi", "core")
Z = ("zhi", "zlo")
GROUP = ("x", "y", "core")
LINE = ("y", "core")
BF16 = jnp.bfloat16
F32 = jnp.float32
I32 = jnp.int32


def owner_of(panel):
    return ((panel >> 2) & 3) * 16 + (panel >> 4) * 4 + (panel & 3)


def place_of(panel):
    return (panel >> 3) * 8 + ((panel >> 1) & 1) * 4 + ((panel >> 2) & 1) * 2 + (panel & 1)


def dot(a, b):
    return lax.dot_general(a, b, (((1,), (0,)), ((), ())), preferred_element_type=F32)


def dot_t(a, b):
    return lax.dot_general(a, b, (((1,), (1,)), ((), ())), preferred_element_type=F32)


def iota(shape, dim):
    return lax.broadcasted_iota(I32, shape, dim)


def one_hot(condition):
    return jnp.where(condition, 1.0, 0.0)


def diagonals(starts, width, stride, rows=ROWS):
    lane, row = iota((ROWS, width), 1), iota((ROWS, width), 0)
    return jnp.concatenate(
        [one_hot((lane - row * stride == start) & (row < rows)) for start in starts], axis=0
    )


def by_tiles(tile_ref, vectors):
    tiles, size = tile_ref.shape[0], tile_ref.shape[1]
    return jnp.concatenate(
        [dot_t(vectors[:, t * size : (t + 1) * size], tile_ref[t]) for t in range(tiles)], axis=1
    ).astype(BF16)


def touched_pieces(corrected, tile_ref, coupling_ref, pack):
    solved = by_tiles(tile_ref, corrected)
    touched = dot_t(solved, coupling_ref[...]).astype(BF16)
    rows = jnp.concatenate([touched[:, s * PANEL : (s + 1) * PANEL] for s in range(PB)], axis=0)
    return dot(pack, rows)


def solve_leaf(rows, corrected_ref, tile_ref, coupling_ref):
    columns = corrected_ref.shape[0]
    picked = jnp.concatenate([rows[s * columns : (s + 1) * columns] for s in range(PB)], axis=1)
    pushed = dot(picked, coupling_ref[...])
    reduced = (corrected_ref[...].astype(F32) - pushed).astype(BF16)
    return by_tiles(tile_ref, reduced)


def unpacker(panels):
    starts = [s * ROWS + c for s in range(panels) for c in range(PER_SET)]
    return diagonals(starts, SETS * panels * ROWS, panels * ROWS).astype(BF16)


def first_kernel(panels_ref, rhs_ref, tile_ref, coupling_ref, out_ref, pack_ref, unpack_ref):
    columns = rhs_ref.shape[0]
    starts = [s * columns + zi for zi in range(SETS) for s in range(PB)]
    pack = diagonals(starts, PB * columns, SETS, PER_SET).astype(BF16)
    pack_ref[...] = pack
    unpack_ref[...] = unpacker(PB)
    pieces = touched_pieces(rhs_ref[...], tile_ref, coupling_ref, pack)
    row = iota(pieces.shape, 0)
    for s in range(PB):
        here = row % (PB * ROWS) == s * ROWS + PER_SET
        pieces = jnp.where(here, panels_ref[0, s].astype(F32), pieces)
    out_ref[...] = pieces.astype(BF16)


def first_spread_kernel(pieces_ref, out_ref, spread_ref, pick_ref):
    rows, cells = pieces_ref.shape[0], spread_ref.shape[0]
    lane, row = iota((rows, rows), 1), iota((rows, rows), 0)
    copy = one_hot((lane // ROWS == row // ROWS) & (lane % ROWS == PER_SET)).astype(BF16)
    numbers = dot(copy, pieces_ref[...])
    down = jnp.concatenate([numbers.astype(I32)] * (cells // PANEL), axis=1)
    lane, row = iota((rows, cells), 1), iota((rows, cells), 0)
    same = (lane % ROWS == row % ROWS) & (row % ROWS < PER_SET)
    pick_ref[...] = one_hot(same & (place_of(down) == lane // ROWS)).astype(BF16)
    corner = one_hot(iota((ROWS, PANEL), 1) == 0).astype(BF16)
    across = dot_t(corner, numbers.astype(BF16)).astype(I32)
    across = jnp.concatenate([owner_of(across)] * (cells // ROWS), axis=0)
    lane, row = iota((cells, rows), 1), iota((cells, rows), 0)
    same = (lane % ROWS == row % ROWS) & (row % ROWS < PER_SET)
    spread = one_hot(same & (across == row // ROWS)).astype(BF16)
    spread_ref[...] = spread
    out_ref[...] = dot(spread, pieces_ref[...]).astype(BF16)


def select_kernel(select_ref, pieces_ref, out_ref):
    out_ref[...] = dot(select_ref[...], pieces_ref[...]).astype(BF16)


def sum_of(pieces_ref):
    total = pieces_ref[0].astype(F32)
    for m in range(1, pieces_ref.shape[0]):
        total = total + pieces_ref[m].astype(F32)
    return total


def copies(out_ref, value):
    for m in range(out_ref.shape[0]):
        out_ref[m] = value


def first_rhs_kernel(pieces_ref, out_ref):
    copies(out_ref, (-sum_of(pieces_ref)).astype(BF16))


def rhs_kernel(where_ref, pieces_ref, step_ref, scale_ref, out_ref):
    step = step_ref[where_ref[1]].astype(F32)
    side = -scale_ref[pl.ds(where_ref[0], 1), :] * step
    copies(out_ref, (side - sum_of(pieces_ref)).astype(BF16))


def step_kernel(pieces_ref, inverse_ref, out_ref):
    rhs = jnp.concatenate([pieces_ref[m] for m in range(pieces_ref.shape[0])], axis=1)
    parts = [dot(rhs, inverse_ref[zh]) for zh in range(2)]
    parts = [part[:, h * PANEL : (h + 1) * PANEL] for part in parts for h in range(2)]
    copies(out_ref, jnp.concatenate(parts, axis=0).astype(BF16))


def total_kernel(pieces_ref, out_ref):
    copies(out_ref, sum_of(pieces_ref).astype(BF16))


def last_total_kernel(pieces_ref, out_ref, own_ref):
    total = sum_of(pieces_ref).astype(BF16)
    copies(out_ref, total)
    own_ref[...] = total


def last_pick_kernel(select_ref, pieces_ref, own_ref, out_ref):
    picked = dot(select_ref[...], pieces_ref[...]).astype(BF16)
    size = picked.shape[0] // SETS
    for zi in range(SETS):
        half = (zi // 4) * 2 * ROWS
        out_ref[zi, :size] = picked[zi * size : (zi + 1) * size]
        out_ref[zi, size:] = own_ref[half : half + 2 * ROWS]


def middle_kernel(
    pieces_ref, unpack_ref, pack_ref, corrected_ref, rhs_ref, scale_ref, tile_ref, coupling_ref,
    out_ref, next_ref,
):
    rows = dot(unpack_ref[...], pieces_ref[...]).astype(BF16)
    leaf = solve_leaf(rows, corrected_ref, tile_ref, coupling_ref)
    corrected = (rhs_ref[...].astype(F32) - scale_ref[...] * leaf.astype(F32)).astype(BF16)
    next_ref[...] = corrected
    out_ref[...] = touched_pieces(corrected, tile_ref, coupling_ref, pack_ref[...]).astype(BF16)


def last_kernel(
    pieces_ref, unpack_ref, corrected_ref, tile_ref, coupling_ref, leaf_ref, link_ref
):
    columns = corrected_ref.shape[0]
    size = PB * ROWS
    pieces = jnp.concatenate([pieces_ref[zi, :size] for zi in range(SETS)], axis=0)
    rows = dot(unpack_ref[...], pieces).astype(BF16)
    leaf_ref[...] = solve_leaf(rows, corrected_ref, tile_ref, coupling_ref)
    link = jnp.concatenate([pieces_ref[zi, size:] for zi in range(SETS)], axis=0)
    link = dot(unpacker(2), link).astype(BF16)
    link_ref[...] = jnp.concatenate([link[:columns], link[columns:]], axis=1)


INTERPRET = False


def call(body, name, shapes, *operands):
    outs = [jax.ShapeDtypeStruct(s, BF16) for s in shapes]
    vmem, smem = (pl.BlockSpec(memory_space=s) for s in (pltpu.VMEM, pltpu.SMEM))
    return pl.pallas_call(
        body,
        name=name,
        out_shape=outs,
        in_specs=[smem if x.dtype == I32 else vmem for x in operands],
        out_specs=[vmem] * len(outs),
        compiler_params=pltpu.CompilerParams(vmem_limit_bytes=24 << 20),
        interpret=INTERPRET,
    )(*operands)


def swap(x, axes):
    return lax.all_to_all(x, axes, 0, 0, tiled=True)


def per_device(
    tile_inverse, link_coupling, link_panels, leaf_rhs, leaf_scale, link_scale, link_inverse
):
    tile_inv, coupling, own_rhs = tile_inverse[0], link_coupling[0], leaf_rhs[0]
    columns = own_rhs.shape[0]
    assert columns == SETS * PER_SET
    x, y, core = lax.axis_index("x"), lax.axis_index("y"), lax.axis_index("core")
    line, members = lax.axis_size(LINE), lax.axis_size(GROUP)

    with jax.named_scope("gather"):
        inverse = lax.all_gather(link_inverse, Z)
        inverse = inverse.reshape(2, -1, link_inverse.shape[1])
    scales = link_scale.reshape(-1, PANEL)
    place = y * 2 + core
    panel = (place >> 2) * 16 + x * 4 + (place & 3)
    where = jnp.stack([panel, place_of(panel)]).astype(I32)

    home = (SETS * PB * ROWS, PANEL)
    flat = (members * ROWS, PANEL)
    mixer = (PB * columns, SETS * PB * ROWS)
    parts = (4 * ROWS, PANEL)
    corrected = own_rhs
    pieces, pack, unpack = call(
        first_kernel, "first", [home, mixer[::-1], mixer], link_panels, own_rhs, tile_inv, coupling
    )
    for solve_index in range(SOLVES):
        last = solve_index == SOLVES - 1
        pieces = swap(pieces.reshape(SETS, PB * ROWS, PANEL), Z).reshape(home)
        if solve_index == 0:
            pieces, spread, pick = call(
                first_spread_kernel, "spread", [flat, (flat[0], home[0]), (home[0], flat[0])], pieces
            )
        else:
            pieces, = call(select_kernel, "spread", [flat], spread, pieces)
        pieces = swap(pieces.reshape(members, ROWS, PANEL), GROUP)
        if solve_index == 0:
            pieces, = call(first_rhs_kernel, "rhs", [(line, ROWS, PANEL)], pieces)
        else:
            pieces, = call(rhs_kernel, "rhs", [(line, ROWS, PANEL)], where, pieces, step, scales)
        pieces = swap(pieces, LINE)
        pieces, = call(step_kernel, "step", [(4,) + parts], pieces, inverse)
        pieces = swap(pieces, "x")
        if last:
            pieces, own = call(last_total_kernel, "total", [(line,) + parts, parts], pieces)
        else:
            pieces, = call(total_kernel, "total", [(line,) + parts], pieces)
        pieces = swap(pieces, LINE)
        step, pieces = pieces.reshape(members, ROWS, PANEL), pieces.reshape(flat)
        if last:
            wide = (SETS, (PB + 2) * ROWS, PANEL)
            pieces, = call(last_pick_kernel, "pick", [wide], pick, pieces, own)
            leaf, link = call(
                last_kernel, "last", [own_rhs.shape, (columns, 2 * PANEL)],
                swap(pieces, Z), unpack, corrected, tile_inv, coupling,
            )
        else:
            pieces, = call(select_kernel, "pick", [home], pick, pieces)
            pieces = swap(pieces.reshape(SETS, PB * ROWS, PANEL), Z).reshape(home)
            pieces, corrected = call(
                middle_kernel, "middle", [home, own_rhs.shape],
                pieces, unpack, pack, corrected, own_rhs, leaf_scale, tile_inv, coupling,
            )
    return leaf[None], link


def solution(mesh):
    fine = Mesh(mesh.devices.reshape(4, 4, 8, 2, 2), SPLIT)
    sec, dev = SPLIT[:2], SPLIT[2:]
    in_specs = (
        P(SPLIT, None, None, None),
        P(SPLIT, None, None),
        P(SPLIT, None),
        P(SPLIT, None, None),
        P(SPLIT, None),
        P(),
        P(sec, dev),
    )
    out_specs = (P(SPLIT, None, None), P(None, dev))
    return jax.shard_map(
        per_device, mesh=fine, in_specs=in_specs, out_specs=out_specs, check_vma=False
    )
```

```python
import jax
import jax.numpy as jnp
from jax import lax
from jax.experimental import pallas as pl
from jax.experimental.pallas import tpu as pltpu
from jax.sharding import Mesh, PartitionSpec as P


PANEL = 128
PB = 4
SOLVES = 5
ROWS = 8
SETS = 8
PER_SET = 6
SPLIT = ("zlo", "x", "y", "zhi", "core")
Z = ("zhi", "zlo")
GROUP = ("x", "y", "core")
LINE = ("y", "core")
BF16 = jnp.bfloat16
F32 = jnp.float32
I32 = jnp.int32


def owner_of(panel):
    return ((panel >> 2) & 3) * 16 + (panel >> 4) * 4 + (panel & 3)


def place_of(panel):
    return (panel >> 3) * 8 + ((panel >> 1) & 1) * 4 + ((panel >> 2) & 1) * 2 + (panel & 1)


def dot(a, b):
    return lax.dot_general(a, b, (((1,), (0,)), ((), ())), preferred_element_type=F32)


def dot_t(a, b):
    return lax.dot_general(a, b, (((1,), (1,)), ((), ())), preferred_element_type=F32)


def iota(shape, dim):
    return lax.broadcasted_iota(I32, shape, dim)


def one_hot(condition):
    return jnp.where(condition, 1.0, 0.0)


def diagonals(starts, width, stride, rows=ROWS):
    lane, row = iota((ROWS, width), 1), iota((ROWS, width), 0)
    return jnp.concatenate(
        [one_hot((lane - row * stride == start) & (row < rows)) for start in starts], axis=0
    )


def by_tiles(tile_ref, vectors):
    tiles, size = tile_ref.shape[0], tile_ref.shape[1]
    return jnp.concatenate(
        [dot_t(vectors[:, t * size : (t + 1) * size], tile_ref[t]) for t in range(tiles)], axis=1
    ).astype(BF16)


def touched_pieces(corrected, tile_ref, coupling_ref, pack):
    solved = by_tiles(tile_ref, corrected)
    touched = dot_t(solved, coupling_ref[...]).astype(BF16)
    rows = jnp.concatenate([touched[:, s * PANEL : (s + 1) * PANEL] for s in range(PB)], axis=0)
    return dot(pack, rows)


def solve_leaf(rows, corrected_ref, tile_ref, coupling_ref):
    columns = corrected_ref.shape[0]
    picked = jnp.concatenate([rows[s * columns : (s + 1) * columns] for s in range(PB)], axis=1)
    pushed = dot(picked, coupling_ref[...])
    reduced = (corrected_ref[...].astype(F32) - pushed).astype(BF16)
    return by_tiles(tile_ref, reduced)


def unpacker(panels):
    starts = [s * ROWS + c for s in range(panels) for c in range(PER_SET)]
    return diagonals(starts, SETS * panels * ROWS, panels * ROWS).astype(BF16)


def first_kernel(
    panels_ref, rhs_hbm, tile_hbm, coupling_hbm, out_ref, pack_ref, unpack_ref,
    rhs_ref, tile_ref, coupling_ref, sems,
):
    columns = rhs_ref.shape[0]
    fetches = [
        pltpu.make_async_copy(rhs_hbm, rhs_ref, sems.at[0]),
        pltpu.make_async_copy(tile_hbm, tile_ref, sems.at[1]),
        pltpu.make_async_copy(coupling_hbm, coupling_ref, sems.at[2]),
    ]
    for fetch in fetches:
        fetch.start()
    starts = [s * columns + zi for zi in range(SETS) for s in range(PB)]
    pack = diagonals(starts, PB * columns, SETS, PER_SET).astype(BF16)
    pack_ref[...] = pack
    unpack_ref[...] = unpacker(PB)
    for fetch in fetches:
        fetch.wait()
    pieces = touched_pieces(rhs_ref[...], tile_ref, coupling_ref, pack)
    row = iota(pieces.shape, 0)
    for s in range(PB):
        here = row % (PB * ROWS) == s * ROWS + PER_SET
        pieces = jnp.where(here, panels_ref[0, s].astype(F32), pieces)
    out_ref[...] = pieces.astype(BF16)


def first_spread_kernel(pieces_ref, out_ref, spread_ref, pick_ref):
    rows, cells = pieces_ref.shape[0], spread_ref.shape[0]
    lane, row = iota((rows, rows), 1), iota((rows, rows), 0)
    copy = one_hot((lane // ROWS == row // ROWS) & (lane % ROWS == PER_SET)).astype(BF16)
    numbers = dot(copy, pieces_ref[...])
    down = jnp.concatenate([numbers.astype(I32)] * (cells // PANEL), axis=1)
    lane, row = iota((rows, cells), 1), iota((rows, cells), 0)
    same = (lane % ROWS == row % ROWS) & (row % ROWS < PER_SET)
    pick_ref[...] = one_hot(same & (place_of(down) == lane // ROWS)).astype(BF16)
    corner = one_hot(iota((ROWS, PANEL), 1) == 0).astype(BF16)
    across = dot_t(corner, numbers.astype(BF16)).astype(I32)
    across = jnp.concatenate([owner_of(across)] * (cells // ROWS), axis=0)
    lane, row = iota((cells, rows), 1), iota((cells, rows), 0)
    same = (lane % ROWS == row % ROWS) & (row % ROWS < PER_SET)
    spread = one_hot(same & (across == row // ROWS)).astype(BF16)
    spread_ref[...] = spread
    out_ref[...] = dot(spread, pieces_ref[...]).astype(BF16)


def select_kernel(select_ref, pieces_ref, out_ref):
    out_ref[...] = dot(select_ref[...], pieces_ref[...]).astype(BF16)


def sum_of(pieces_ref):
    total = pieces_ref[0].astype(F32)
    for m in range(1, pieces_ref.shape[0]):
        total = total + pieces_ref[m].astype(F32)
    return total


def copies(out_ref, value):
    for m in range(out_ref.shape[0]):
        out_ref[m] = value


def first_rhs_kernel(pieces_ref, out_ref):
    copies(out_ref, (-sum_of(pieces_ref)).astype(BF16))


def rhs_kernel(where_ref, pieces_ref, step_ref, scale_ref, out_ref):
    step = step_ref[where_ref[1]].astype(F32)
    side = -scale_ref[pl.ds(where_ref[0], 1), :] * step
    copies(out_ref, (side - sum_of(pieces_ref)).astype(BF16))


def step_kernel(pieces_ref, inverse_ref, out_ref):
    rhs = jnp.concatenate([pieces_ref[m] for m in range(pieces_ref.shape[0])], axis=1)
    parts = [dot(rhs, inverse_ref[zh]) for zh in range(2)]
    parts = [part[:, h * PANEL : (h + 1) * PANEL] for part in parts for h in range(2)]
    copies(out_ref, jnp.concatenate(parts, axis=0).astype(BF16))


def total_kernel(pieces_ref, out_ref):
    copies(out_ref, sum_of(pieces_ref).astype(BF16))


def last_total_kernel(pieces_ref, out_ref, own_ref):
    total = sum_of(pieces_ref).astype(BF16)
    copies(out_ref, total)
    own_ref[...] = total


def last_pick_kernel(select_ref, pieces_ref, own_ref, out_ref):
    picked = dot(select_ref[...], pieces_ref[...]).astype(BF16)
    size = picked.shape[0] // SETS
    for zi in range(SETS):
        half = (zi // 4) * 2 * ROWS
        out_ref[zi, :size] = picked[zi * size : (zi + 1) * size]
        out_ref[zi, size:] = own_ref[half : half + 2 * ROWS]


def correct(rhs_ref, scale_ref, leaf):
    return (rhs_ref[...].astype(F32) - scale_ref[...] * leaf.astype(F32)).astype(BF16)


def ahead_pieces(corrected, rhs_ref, scale_ref, tile_ref, coupling_ref, pack):
    leaf = by_tiles(tile_ref, corrected)
    return touched_pieces(correct(rhs_ref, scale_ref, leaf), tile_ref, coupling_ref, pack)


def response_kernel(after_ref, scale_ref, tile_ref, coupling_ref, out_ref):
    leaf = by_tiles(tile_ref, coupling_ref[...])
    moved = (scale_ref[...] * leaf.astype(F32)).astype(BF16)
    solved = by_tiles(tile_ref, moved)
    out_ref[...] = dot_t(solved, coupling_ref[...]).astype(BF16)


def middle_kernel(
    pieces_ref, unpack_ref, pack_ref, corrected_ref, rhs_ref, scale_ref, tile_ref, coupling_ref,
    out_ref, next_ref,
):
    rows = dot(unpack_ref[...], pieces_ref[...]).astype(BF16)
    leaf = solve_leaf(rows, corrected_ref, tile_ref, coupling_ref)
    corrected = correct(rhs_ref, scale_ref, leaf)
    next_ref[...] = corrected
    out_ref[...] = touched_pieces(corrected, tile_ref, coupling_ref, pack_ref[...]).astype(BF16)


def ahead_kernel(
    pack_ref, corrected_ref, rhs_ref, scale_ref, tile_ref, coupling_ref, out_ref
):
    out_ref[...] = ahead_pieces(
        corrected_ref[...], rhs_ref, scale_ref, tile_ref, coupling_ref, pack_ref[...]
    ).astype(BF16)


def home_kernel(
    pieces_ref, unpack_ref, corrected_ref, rhs_ref, scale_ref, tile_ref, coupling_ref, next_ref
):
    size = PB * ROWS
    pieces = jnp.concatenate([pieces_ref[zi, :size] for zi in range(SETS)], axis=0)
    rows = dot(unpack_ref[...], pieces).astype(BF16)
    leaf = solve_leaf(rows, corrected_ref, tile_ref, coupling_ref)
    next_ref[...] = correct(rhs_ref, scale_ref, leaf)


def both_pick_kernel(select_ref, pieces_ref, ahead_ref, out_ref, picked_ref):
    picked = dot(select_ref[...], pieces_ref[...]).astype(BF16)
    picked_ref[...] = picked
    size = PB * ROWS
    for zi in range(SETS):
        out_ref[zi, :size] = picked[zi * size : (zi + 1) * size]
        out_ref[zi, size:] = ahead_ref[zi * size : (zi + 1) * size]


def respond_kernel(pieces_ref, picked_ref, spread_ref, response_hbm, out_ref, response_ref, sems):
    size, rows = PB * ROWS, []
    fetches = [
        pltpu.make_async_copy(response_hbm.at[zi], response_ref.at[zi], sems.at[zi])
        for zi in range(SETS)
    ]
    for fetch in fetches:
        fetch.start()
    for zi in range(SETS):
        places = [slice(s * ROWS, (s + 1) * ROWS) for s in range(PB)]
        picked = jnp.concatenate([picked_ref[zi * size + p.start : zi * size + p.stop] for p in places], axis=1)
        fetches[zi].wait()
        added = dot(picked, response_ref[zi])
        added = jnp.concatenate([added[:, s * PANEL : (s + 1) * PANEL] for s in range(PB)], axis=0)
        rows.append((pieces_ref[zi, size:].astype(F32) + added).astype(BF16))
    out_ref[...] = dot(spread_ref[...], jnp.concatenate(rows, axis=0)).astype(BF16)


def last_kernel(
    pieces_ref, unpack_ref, corrected_ref, tile_ref, coupling_ref, leaf_ref, link_ref
):
    columns = corrected_ref.shape[0]
    size = PB * ROWS
    pieces = jnp.concatenate([pieces_ref[zi, :size] for zi in range(SETS)], axis=0)
    rows = dot(unpack_ref[...], pieces).astype(BF16)
    leaf_ref[...] = solve_leaf(rows, corrected_ref, tile_ref, coupling_ref)
    link = jnp.concatenate([pieces_ref[zi, size:] for zi in range(SETS)], axis=0)
    link = dot(unpacker(2), link).astype(BF16)
    link_ref[...] = jnp.concatenate([link[:columns], link[columns:]], axis=1)


INTERPRET = False


def call(body, shapes, *operands, fetched=()):
    outs = [jax.ShapeDtypeStruct(s, BF16) for s in shapes]
    vmem, smem, anywhere = (
        pl.BlockSpec(memory_space=s) for s in (pltpu.VMEM, pltpu.SMEM, pltpu.HBM)
    )
    operands = [
        pltpu.with_memory_space_constraint(x, pltpu.HBM) if i in fetched and not INTERPRET else x
        for i, x in enumerate(operands)
    ]
    scratch = [pltpu.VMEM(operands[i].shape, BF16) for i in fetched]
    if fetched:
        scratch.append(pltpu.SemaphoreType.DMA((SETS,)))
    return pl.pallas_call(
        body,
        out_shape=outs,
        in_specs=[
            anywhere if i in fetched else smem if x.dtype == I32 else vmem
            for i, x in enumerate(operands)
        ],
        out_specs=[vmem] * len(outs),
        scratch_shapes=scratch,
        compiler_params=pltpu.CompilerParams(vmem_limit_bytes=24 << 20),
        interpret=INTERPRET,
    )(*operands)


def swap(x, axes):
    return lax.all_to_all(x, axes, 0, 0, tiled=True)


def per_device(
    tile_inverse, link_coupling, link_panels, leaf_rhs, leaf_scale, link_scale, link_inverse
):
    tile_inv, coupling, own_rhs = tile_inverse[0], link_coupling[0], leaf_rhs[0]
    columns = own_rhs.shape[0]
    assert columns == SETS * PER_SET
    x, y, core = lax.axis_index("x"), lax.axis_index("y"), lax.axis_index("core")
    line, members = lax.axis_size(LINE), lax.axis_size(GROUP)

    inverse = lax.all_gather(link_inverse, Z)
    inverse = inverse.reshape(2, -1, link_inverse.shape[1])
    scales = link_scale.reshape(-1, PANEL)
    place = y * 2 + core
    panel = (place >> 2) * 16 + x * 4 + (place & 3)
    where = jnp.stack([panel, place_of(panel)]).astype(I32)

    home = (SETS * PB * ROWS, PANEL)
    flat = (members * ROWS, PANEL)
    mixer = (PB * columns, SETS * PB * ROWS)
    parts = (4 * ROWS, PANEL)
    corrected = own_rhs
    pieces, pack, unpack = call(
        first_kernel, [home, mixer[::-1], mixer], link_panels, own_rhs, tile_inv, coupling,
        fetched=(1, 2, 3),
    )
    for solve_index in range(SOLVES):
        last = solve_index == SOLVES - 1
        if solve_index < 2:
            pieces = swap(pieces.reshape(SETS, PB * ROWS, PANEL), Z).reshape(home)
        if solve_index == 0:
            pieces, spread, pick = call(
                first_spread_kernel, [flat, (flat[0], home[0]), (home[0], flat[0])], pieces
            )
            response, = call(
                response_kernel, [(PB * PANEL,) * 2],
                pieces, leaf_scale, tile_inv, coupling,
            )
            response = lax.all_gather(response, Z)
        elif solve_index == 1:
            pieces, = call(select_kernel, [flat], spread, pieces)
        else:
            pieces, = call(respond_kernel, [flat], both, picked, spread, response, fetched=(3,))
        pieces = swap(pieces.reshape(members, ROWS, PANEL), GROUP)
        if solve_index == 0:
            pieces, = call(first_rhs_kernel, [(line, ROWS, PANEL)], pieces)
        else:
            pieces, = call(rhs_kernel, [(line, ROWS, PANEL)], where, pieces, step, scales)
        pieces = swap(pieces, LINE)
        pieces, = call(step_kernel, [(4,) + parts], pieces, inverse)
        pieces = swap(pieces, "x")
        if last:
            pieces, own = call(last_total_kernel, [(line,) + parts, parts], pieces)
        else:
            pieces, = call(total_kernel, [(line,) + parts], pieces)
        pieces = swap(pieces, LINE)
        step, pieces = pieces.reshape(members, ROWS, PANEL), pieces.reshape(flat)
        if last:
            wide = (SETS, (PB + 2) * ROWS, PANEL)
            pieces, = call(last_pick_kernel, [wide], pick, pieces, own)
            leaf, link = call(
                last_kernel, [own_rhs.shape, (columns, 2 * PANEL)],
                swap(pieces, Z), unpack, corrected, tile_inv, coupling,
            )
        elif solve_index == 0:
            pieces, = call(select_kernel, [home], pick, pieces)
            pieces = swap(pieces.reshape(SETS, PB * ROWS, PANEL), Z).reshape(home)
            pieces, corrected = call(
                middle_kernel, [home, own_rhs.shape],
                pieces, unpack, pack, corrected, own_rhs, leaf_scale, tile_inv, coupling,
            )
        else:
            both = (SETS, 2 * PB * ROWS, PANEL)
            ahead, = call(
                ahead_kernel, [home],
                pack, corrected, own_rhs, leaf_scale, tile_inv, coupling,
            )
            both, picked = call(both_pick_kernel, [both, home], pick, pieces, ahead)
            both = swap(both, Z)
            corrected, = call(
                home_kernel, [own_rhs.shape],
                both, unpack, corrected, own_rhs, leaf_scale, tile_inv, coupling,
            )
    return leaf[None], link


def solution(mesh):
    fine = Mesh(mesh.devices.reshape(4, 4, 8, 2, 2), SPLIT)
    sec, dev = SPLIT[:2], SPLIT[2:]
    in_specs = (
        P(SPLIT, None, None, None),
        P(SPLIT, None, None),
        P(SPLIT, None),
        P(SPLIT, None, None),
        P(SPLIT, None),
        P(),
        P(sec, dev),
    )
    out_specs = (P(SPLIT, None, None), P(None, dev))
    return jax.shard_map(
        per_device, mesh=fine, in_specs=in_specs, out_specs=out_specs, check_vma=False
    )
```

```python
import jax
import jax.numpy as jnp
from jax import lax
from jax.experimental import pallas as pl
from jax.experimental.pallas import tpu as pltpu
from jax.sharding import Mesh, PartitionSpec as P


PANEL = 128
PB = 4
SOLVES = 5
ROWS = 8
SETS = 8
PER_SET = 6
SPLIT = ("zlo", "x", "y", "zhi", "core")
Z = ("zhi", "zlo")
GROUP = ("x", "y", "core")
LINE = ("y", "core")
BF16 = jnp.bfloat16
F32 = jnp.float32
I32 = jnp.int32


def owner_of(panel):
    return ((panel >> 2) & 3) * 16 + (panel >> 4) * 4 + (panel & 3)


def place_of(panel):
    return (panel >> 3) * 8 + ((panel >> 1) & 1) * 4 + ((panel >> 2) & 1) * 2 + (panel & 1)


def dot(a, b):
    return lax.dot_general(a, b, (((1,), (0,)), ((), ())), preferred_element_type=F32)


def dot_t(a, b):
    return lax.dot_general(a, b, (((1,), (1,)), ((), ())), preferred_element_type=F32)


def iota(shape, dim):
    return lax.broadcasted_iota(I32, shape, dim)


def one_hot(condition):
    return jnp.where(condition, 1.0, 0.0)


def diagonals(starts, width, stride, rows=ROWS):
    lane, row = iota((ROWS, width), 1), iota((ROWS, width), 0)
    return jnp.concatenate(
        [one_hot((lane - row * stride == start) & (row < rows)) for start in starts], axis=0
    )


def by_tiles(tile_ref, vectors):
    tiles, size = tile_ref.shape[0], tile_ref.shape[1]
    return jnp.concatenate(
        [dot_t(vectors[:, t * size : (t + 1) * size], tile_ref[t]) for t in range(tiles)], axis=1
    ).astype(BF16)


def touched_pieces(solved, coupling_ref, pack):
    touched = dot_t(solved, coupling_ref[...]).astype(BF16)
    rows = jnp.concatenate([touched[:, s * PANEL : (s + 1) * PANEL] for s in range(PB)], axis=0)
    return dot(pack, rows)


def solve_leaf(rows, corrected, tile_ref, coupling_ref):
    columns = corrected.shape[0]
    picked = jnp.concatenate([rows[s * columns : (s + 1) * columns] for s in range(PB)], axis=1)
    pushed = dot(picked, coupling_ref[...])
    reduced = (corrected.astype(F32) - pushed).astype(BF16)
    return by_tiles(tile_ref, reduced)


def unpacker(panels):
    starts = [s * ROWS + c for s in range(panels) for c in range(PER_SET)]
    return diagonals(starts, SETS * panels * ROWS, panels * ROWS).astype(BF16)


def first_kernel(
    panels_ref, rhs_hbm, tile_hbm, coupling_hbm, out_ref, pack_ref, unpack_ref,
    rhs_ref, tile_ref, coupling_ref, sems,
):
    columns = rhs_ref.shape[0]
    fetches = [
        pltpu.make_async_copy(rhs_hbm, rhs_ref, sems.at[0]),
        pltpu.make_async_copy(tile_hbm, tile_ref, sems.at[1]),
        pltpu.make_async_copy(coupling_hbm, coupling_ref, sems.at[2]),
    ]
    for fetch in fetches:
        fetch.start()
    starts = [s * columns + zi for zi in range(SETS) for s in range(PB)]
    pack = diagonals(starts, PB * columns, SETS, PER_SET).astype(BF16)
    pack_ref[...] = pack
    unpack_ref[...] = unpacker(PB)
    for fetch in fetches:
        fetch.wait()
    pieces = touched_pieces(by_tiles(tile_ref, rhs_ref[...]), coupling_ref, pack)
    row = iota(pieces.shape, 0)
    for s in range(PB):
        here = row % (PB * ROWS) == s * ROWS + PER_SET
        pieces = jnp.where(here, panels_ref[0, s].astype(F32), pieces)
    out_ref[...] = pieces.astype(BF16)


def first_spread_kernel(pieces_ref, out_ref, spread_ref, pick_ref):
    rows, cells = pieces_ref.shape[0], spread_ref.shape[0]
    lane, row = iota((rows, rows), 1), iota((rows, rows), 0)
    copy = one_hot((lane // ROWS == row // ROWS) & (lane % ROWS == PER_SET)).astype(BF16)
    numbers = dot(copy, pieces_ref[...])
    down = jnp.concatenate([numbers.astype(I32)] * (cells // PANEL), axis=1)
    lane, row = iota((rows, cells), 1), iota((rows, cells), 0)
    same = (lane % ROWS == row % ROWS) & (row % ROWS < PER_SET)
    pick_ref[...] = one_hot(same & (place_of(down) == lane // ROWS)).astype(BF16)
    corner = one_hot(iota((ROWS, PANEL), 1) == 0).astype(BF16)
    across = dot_t(corner, numbers.astype(BF16)).astype(I32)
    across = jnp.concatenate([owner_of(across)] * (cells // ROWS), axis=0)
    lane, row = iota((cells, rows), 1), iota((cells, rows), 0)
    same = (lane % ROWS == row % ROWS) & (row % ROWS < PER_SET)
    spread = one_hot(same & (across == row // ROWS)).astype(BF16)
    spread_ref[...] = spread
    out_ref[...] = dot(spread, pieces_ref[...]).astype(BF16)


def select_kernel(select_ref, pieces_ref, out_ref):
    out_ref[...] = dot(select_ref[...], pieces_ref[...]).astype(BF16)


def sum_of(pieces_ref):
    total = pieces_ref[0].astype(F32)
    for m in range(1, pieces_ref.shape[0]):
        total = total + pieces_ref[m].astype(F32)
    return total


def copies(out_ref, value):
    for m in range(out_ref.shape[0]):
        out_ref[m] = value


def first_rhs_kernel(pieces_ref, out_ref):
    copies(out_ref, (-sum_of(pieces_ref)).astype(BF16))


def rhs_kernel(where_ref, pieces_ref, step_ref, scale_ref, out_ref):
    step = step_ref[where_ref[1]].astype(F32)
    side = -scale_ref[pl.ds(where_ref[0], 1), :] * step
    copies(out_ref, (side - sum_of(pieces_ref)).astype(BF16))


def step_kernel(pieces_ref, inverse_ref, out_ref):
    rhs = jnp.concatenate([pieces_ref[m] for m in range(pieces_ref.shape[0])], axis=1)
    parts = [dot(rhs, inverse_ref[zh]) for zh in range(2)]
    parts = [part[:, h * PANEL : (h + 1) * PANEL] for part in parts for h in range(2)]
    copies(out_ref, jnp.concatenate(parts, axis=0).astype(BF16))


def total_kernel(pieces_ref, out_ref):
    copies(out_ref, sum_of(pieces_ref).astype(BF16))


def last_total_kernel(pieces_ref, out_ref, own_ref):
    total = sum_of(pieces_ref).astype(BF16)
    copies(out_ref, total)
    own_ref[...] = total


def last_pick_kernel(select_ref, pieces_ref, own_ref, *refs):
    out_ref, size = refs[-1], PB * ROWS
    picked = [ref[...] for ref in refs[:-1]]
    picked.append(dot(select_ref[...], pieces_ref[...]).astype(BF16))
    for zi in range(SETS):
        half = (zi // 4) * 2 * ROWS
        for k, rows in enumerate(picked):
            out_ref[zi, k * size : (k + 1) * size] = rows[zi * size : (zi + 1) * size]
        out_ref[zi, len(picked) * size :] = own_ref[half : half + 2 * ROWS]


def correct(rhs_ref, scale_ref, leaf):
    return (rhs_ref[...].astype(F32) - scale_ref[...] * leaf.astype(F32)).astype(BF16)


def in_chunks(body, rows, chunk=256):
    def step(i, carry):
        body(pl.ds(pl.multiple_of(i * chunk, chunk), chunk))
        return carry

    lax.fori_loop(0, rows // chunk, step, 0)


def first_response_kernel(after_ref, scale_ref, tile_ref, coupling_ref, out_ref, solved_ref):
    def some(rows):
        leaf = by_tiles(tile_ref, coupling_ref[rows, :])
        solved = by_tiles(tile_ref, (scale_ref[...] * leaf.astype(F32)).astype(BF16))
        solved_ref[rows, :] = solved
        out_ref[rows, :] = dot_t(solved, coupling_ref[...]).astype(BF16)

    in_chunks(some, out_ref.shape[0])


def response_kernel(after_ref, earlier_ref, scale_ref, tile_ref, coupling_ref, out_ref, solved_ref):
    def some(rows):
        moved = (-scale_ref[...] * earlier_ref[rows, :].astype(F32)).astype(BF16)
        solved = by_tiles(tile_ref, moved)
        solved_ref[rows, :] = solved
        out_ref[rows, :] = dot_t(solved, coupling_ref[...]).astype(BF16)

    in_chunks(some, out_ref.shape[0])


def ahead_kernel(
    pieces_ref, unpack_ref, pack_ref, rhs_ref, scale_ref, tile_ref, coupling_ref,
    out_ref, next_ref, state_ref,
):
    size = PB * ROWS
    rows = dot(unpack_ref[...], pieces_ref[...]).astype(BF16)
    leaf = solve_leaf(rows, rhs_ref[...], tile_ref, coupling_ref)
    corrected = correct(rhs_ref, scale_ref, leaf)
    next_ref[...] = corrected
    state_ref[...] = corrected

    def solve(k, carry):
        solved = by_tiles(tile_ref, state_ref[...])
        state_ref[...] = correct(rhs_ref, scale_ref, solved)
        pieces = touched_pieces(solved, coupling_ref, pack_ref[...]).astype(BF16)
        rows = pl.ds(pl.multiple_of(k * size, size), size)
        for zi in range(SETS):
            out_ref[zi, rows, :] = pieces[zi * size : (zi + 1) * size]
        return carry

    lax.fori_loop(0, SOLVES - 1, solve, 0)


def ahead_rows(ahead_ref, k):
    size = PB * ROWS
    return jnp.concatenate(
        [ahead_ref[zi, (k - 1) * size : k * size] for zi in range(SETS)], axis=0
    )


def ahead_spread_kernel(spread_ref, ahead_ref, out_ref):
    out_ref[...] = dot(spread_ref[...], ahead_rows(ahead_ref, 1)).astype(BF16)


def fetch_all(response_hbm, response_ref, sems):
    fetches = [
        pltpu.make_async_copy(response_hbm.at[zi], response_ref.at[zi], sems.at[zi])
        for zi in range(SETS)
    ]
    for fetch in fetches:
        fetch.start()
    return fetches


def responses(fetches, picked_ref, response_ref):
    rows = []
    for zi in range(SETS):
        starts = [(zi * PB + s) * ROWS for s in range(PB)]
        picked = jnp.concatenate([picked_ref[r : r + ROWS] for r in starts], axis=1)
        fetches[zi].wait()
        added = dot(picked, response_ref[zi])
        rows += [added[:, s * PANEL : (s + 1) * PANEL] for s in range(PB)]
    return jnp.concatenate(rows, axis=0)


def respond_kernel(base_ref, picked_ref, spread_ref, response_hbm, out_ref, response_ref, sems):
    fetches = fetch_all(response_hbm, response_ref, sems)
    base = ahead_rows(base_ref, 2) if base_ref.ndim == 3 else base_ref[...]
    touched = base.astype(F32) + responses(fetches, picked_ref, response_ref)
    out_ref[...] = dot(spread_ref[...], touched.astype(BF16)).astype(BF16)


def third_base_kernel(ahead_ref, picked_ref, response_hbm, out_ref, response_ref, sems):
    fetches = fetch_all(response_hbm, response_ref, sems)
    added = responses(fetches, picked_ref, response_ref)
    out_ref[...] = ahead_rows(ahead_ref, 3).astype(F32) + added


def fourth_base_kernel(
    ahead_ref, near_ref, far_ref, near_hbm, far_hbm, out_ref,
    near_response_ref, far_response_ref, near_sems, far_sems,
):
    near = fetch_all(near_hbm, near_response_ref, near_sems)
    far = fetch_all(far_hbm, far_response_ref, far_sems)
    added = responses(near, near_ref, near_response_ref)
    added = added + responses(far, far_ref, far_response_ref)
    out_ref[...] = ahead_rows(ahead_ref, 4).astype(F32) + added


def last_kernel(
    pieces_ref, unpack_ref, corrected_ref, rhs_ref, scale_ref, tile_ref, coupling_ref,
    leaf_ref, link_ref, state_ref,
):
    columns, size = corrected_ref.shape[0], PB * ROWS
    state_ref[...] = corrected_ref[...]

    def solve(k, carry):
        at = pl.ds(pl.multiple_of(k * size, size), size)
        pieces = jnp.concatenate([pieces_ref[zi, at, :] for zi in range(SETS)], axis=0)
        rows = dot(unpack_ref[...], pieces).astype(BF16)
        leaf = solve_leaf(rows, state_ref[...], tile_ref, coupling_ref)
        leaf_ref[...] = leaf
        state_ref[...] = correct(rhs_ref, scale_ref, leaf)
        return carry

    lax.fori_loop(0, SOLVES - 1, solve, 0)
    link = jnp.concatenate([pieces_ref[zi, (SOLVES - 1) * size :] for zi in range(SETS)], axis=0)
    link = dot(unpacker(2), link).astype(BF16)
    link_ref[...] = jnp.concatenate([link[:columns], link[columns:]], axis=1)


INTERPRET = False


def call(body, shapes, *operands, fetched=(), queues=1, state=(), dtype=BF16):
    outs = [jax.ShapeDtypeStruct(s, dtype) for s in shapes]
    vmem, smem, anywhere = (
        pl.BlockSpec(memory_space=s) for s in (pltpu.VMEM, pltpu.SMEM, pltpu.HBM)
    )
    operands = [
        pltpu.with_memory_space_constraint(x, pltpu.HBM) if i in fetched and not INTERPRET else x
        for i, x in enumerate(operands)
    ]
    scratch = [pltpu.VMEM(s, BF16) for s in state]
    scratch += [pltpu.VMEM(operands[i].shape, BF16) for i in fetched]
    if fetched:
        scratch += [pltpu.SemaphoreType.DMA((SETS,))] * queues
    return pl.pallas_call(
        body,
        out_shape=outs,
        in_specs=[
            anywhere if i in fetched else smem if x.dtype == I32 else vmem
            for i, x in enumerate(operands)
        ],
        out_specs=[vmem] * len(outs),
        scratch_shapes=scratch,
        compiler_params=pltpu.CompilerParams(vmem_limit_bytes=24 << 20),
        interpret=INTERPRET,
    )(*operands)


def swap(x, axes):
    return lax.all_to_all(x, axes, 0, 0, tiled=True)


def per_device(
    tile_inverse, link_coupling, link_panels, leaf_rhs, leaf_scale, link_scale, link_inverse
):
    tile_inv, coupling, own_rhs = tile_inverse[0], link_coupling[0], leaf_rhs[0]
    columns = own_rhs.shape[0]
    assert columns == SETS * PER_SET
    x, y, core = lax.axis_index("x"), lax.axis_index("y"), lax.axis_index("core")
    line, members = lax.axis_size(LINE), lax.axis_size(GROUP)

    inverse = lax.all_gather(link_inverse, Z)
    inverse = inverse.reshape(2, -1, link_inverse.shape[1])
    scales = link_scale.reshape(-1, PANEL)
    place = y * 2 + core
    panel = (place >> 2) * 16 + x * 4 + (place & 3)
    where = jnp.stack([panel, place_of(panel)]).astype(I32)

    home = (SETS * PB * ROWS, PANEL)
    flat = (members * ROWS, PANEL)
    mixer = (PB * columns, SETS * PB * ROWS)
    parts = (4 * ROWS, PANEL)
    pieces, pack, unpack = call(
        first_kernel, [home, mixer[::-1], mixer], link_panels, own_rhs, tile_inv, coupling,
        fetched=(1, 2, 3),
    )
    sent = (SETS, PB * ROWS, PANEL)
    blocks = (leaf_scale, tile_inv, coupling)
    answers, picks = [], []
    for k in range(SOLVES):
        last = k == SOLVES - 1
        if k == 0:
            pieces, spread, pick = call(
                first_spread_kernel, [flat, (flat[0], home[0]), (home[0], flat[0])],
                swap(pieces.reshape(sent), Z).reshape(home),
            )
        elif k == 1:
            pieces, = call(ahead_spread_kernel, [flat], spread, ahead)
        else:
            base = ahead if k == 2 else base
            pieces, = call(
                respond_kernel, [flat], base, picks[-1], spread, answers[0], fetched=(3,)
            )
        if k < 3:
            answer = [(PB * PANEL,) * 2, (PB * PANEL, own_rhs.shape[1])]
            if k == 0:
                answer, solved = call(first_response_kernel, answer, pieces, *blocks)
            else:
                answer, solved = call(response_kernel, answer, pieces, solved, *blocks)
            answers.append(lax.all_gather(answer, Z))
        pieces = swap(pieces.reshape(members, ROWS, PANEL), GROUP)
        if k == 0:
            pieces, = call(first_rhs_kernel, [(line, ROWS, PANEL)], pieces)
        else:
            pieces, = call(rhs_kernel, [(line, ROWS, PANEL)], where, pieces, step, scales)
        pieces = swap(pieces, LINE)
        pieces, = call(step_kernel, [(4,) + parts], pieces, inverse)
        pieces = swap(pieces, "x")
        if last:
            pieces, own = call(last_total_kernel, [(line,) + parts, parts], pieces)
        else:
            pieces, = call(total_kernel, [(line,) + parts], pieces)
        pieces = swap(pieces, LINE)
        if k == 2:
            base, = call(
                third_base_kernel, [home], ahead, picks[0], answers[1],
                fetched=(2,), dtype=F32,
            )
        elif k == 3:
            base, = call(
                fourth_base_kernel, [home],
                ahead, picks[1], picks[0], answers[1], answers[2],
                fetched=(3, 4), queues=2, dtype=F32,
            )
        step, pieces = pieces.reshape(members, ROWS, PANEL), pieces.reshape(flat)
        if last:
            wide = (SETS, ((SOLVES - 1) * PB + 2) * ROWS, PANEL)
            pieces, = call(last_pick_kernel, [wide], pick, pieces, own, *picks)
            leaf, link = call(
                last_kernel, [own_rhs.shape, (columns, 2 * PANEL)],
                swap(pieces, Z), unpack, corrected, own_rhs, *blocks, state=(own_rhs.shape,),
            )
        else:
            picked, = call(select_kernel, [home], pick, pieces)
            if k == 0:
                ahead, corrected = call(
                    ahead_kernel, [(SETS, (SOLVES - 1) * PB * ROWS, PANEL), own_rhs.shape],
                    swap(picked.reshape(sent), Z).reshape(home),
                    unpack, pack, own_rhs, *blocks, state=(own_rhs.shape,),
                )
                ahead = swap(ahead, Z)
            else:
                picks.append(picked)
    return leaf[None], link


def solution(mesh):
    fine = Mesh(mesh.devices.reshape(4, 4, 8, 2, 2), SPLIT)
    sec, dev = SPLIT[:2], SPLIT[2:]
    in_specs = (
        P(SPLIT, None, None, None),
        P(SPLIT, None, None),
        P(SPLIT, None),
        P(SPLIT, None, None),
        P(SPLIT, None),
        P(),
        P(sec, dev),
    )
    out_specs = (P(SPLIT, None, None), P(None, dev))
    return jax.shard_map(
        per_device, mesh=fine, in_specs=in_specs, out_specs=out_specs, check_vma=False
    )
```

```python
import jax
import jax.numpy as jnp
from jax import lax
from jax.experimental import pallas as pl
from jax.experimental.pallas import tpu as pltpu
from jax.sharding import Mesh, PartitionSpec as P


PANEL = 128
PB = 4
SOLVES = 5
ROWS = 8
SETS = 8
PER_SET = 6
SPLIT = ("zlo", "x", "y", "zhi", "core")
Z = ("zhi", "zlo")
GROUP = ("x", "y", "core")
LINE = ("y", "core")
BF16 = jnp.bfloat16
F32 = jnp.float32
I32 = jnp.int32


def owner_of(panel):
    return ((panel >> 2) & 3) * 16 + (panel >> 4) * 4 + (panel & 3)


def place_of(panel):
    return (panel >> 3) * 8 + ((panel >> 1) & 1) * 4 + ((panel >> 2) & 1) * 2 + (panel & 1)


def dot(a, b):
    return lax.dot_general(a, b, (((1,), (0,)), ((), ())), preferred_element_type=F32)


def dot_t(a, b):
    return lax.dot_general(a, b, (((1,), (1,)), ((), ())), preferred_element_type=F32)


def iota(shape, dim):
    return lax.broadcasted_iota(I32, shape, dim)


def one_hot(condition):
    return jnp.where(condition, 1.0, 0.0)


def diagonals(starts, width, stride, rows=ROWS):
    lane, row = iota((ROWS, width), 1), iota((ROWS, width), 0)
    return jnp.concatenate(
        [one_hot((lane - row * stride == start) & (row < rows)) for start in starts], axis=0
    )


def by_tiles(tile_ref, vectors):
    tiles, size = tile_ref.shape[0], tile_ref.shape[1]
    return jnp.concatenate(
        [dot_t(vectors[:, t * size : (t + 1) * size], tile_ref[t]) for t in range(tiles)], axis=1
    ).astype(BF16)


def touched_pieces(solved, coupling_ref, pack):
    touched = dot_t(solved, coupling_ref[...]).astype(BF16)
    rows = jnp.concatenate([touched[:, s * PANEL : (s + 1) * PANEL] for s in range(PB)], axis=0)
    return dot(pack, rows)


def solve_leaf(rows, corrected, tile_ref, coupling_ref):
    columns = corrected.shape[0]
    picked = jnp.concatenate([rows[s * columns : (s + 1) * columns] for s in range(PB)], axis=1)
    pushed = dot(picked, coupling_ref[...])
    reduced = (corrected.astype(F32) - pushed).astype(BF16)
    return by_tiles(tile_ref, reduced)


def unpacker(panels):
    starts = [s * ROWS + c for s in range(panels) for c in range(PER_SET)]
    return diagonals(starts, SETS * panels * ROWS, panels * ROWS).astype(BF16)


def first_kernel(
    panels_ref, rhs_hbm, tile_hbm, coupling_hbm, out_ref, pack_ref, unpack_ref,
    rhs_ref, tile_ref, coupling_ref, sems,
):
    columns = rhs_ref.shape[0]
    fetches = [
        pltpu.make_async_copy(rhs_hbm, rhs_ref, sems.at[0]),
        pltpu.make_async_copy(tile_hbm, tile_ref, sems.at[1]),
        pltpu.make_async_copy(coupling_hbm, coupling_ref, sems.at[2]),
    ]
    for fetch in fetches:
        fetch.start()
    starts = [s * columns + zi for zi in range(SETS) for s in range(PB)]
    pack = diagonals(starts, PB * columns, SETS, PER_SET).astype(BF16)
    pack_ref[...] = pack
    unpack_ref[...] = unpacker(PB)
    for fetch in fetches:
        fetch.wait()
    pieces = touched_pieces(by_tiles(tile_ref, rhs_ref[...]), coupling_ref, pack)
    row = iota(pieces.shape, 0)
    for s in range(PB):
        here = row % (PB * ROWS) == s * ROWS + PER_SET
        pieces = jnp.where(here, panels_ref[0, s].astype(F32), pieces)
    out_ref[...] = pieces.astype(BF16)


def first_spread_kernel(pieces_ref, out_ref, spread_ref, pick_ref):
    rows, cells = pieces_ref.shape[0], spread_ref.shape[0]
    lane, row = iota((rows, rows), 1), iota((rows, rows), 0)
    copy = one_hot((lane // ROWS == row // ROWS) & (lane % ROWS == PER_SET)).astype(BF16)
    numbers = dot(copy, pieces_ref[...])
    down = jnp.concatenate([numbers.astype(I32)] * (cells // PANEL), axis=1)
    lane, row = iota((rows, cells), 1), iota((rows, cells), 0)
    same = (lane % ROWS == row % ROWS) & (row % ROWS < PER_SET)
    pick_ref[...] = one_hot(same & (place_of(down) == lane // ROWS)).astype(BF16)
    corner = one_hot(iota((ROWS, PANEL), 1) == 0).astype(BF16)
    across = dot_t(corner, numbers.astype(BF16)).astype(I32)
    across = jnp.concatenate([owner_of(across)] * (cells // ROWS), axis=0)
    lane, row = iota((cells, rows), 1), iota((cells, rows), 0)
    same = (lane % ROWS == row % ROWS) & (row % ROWS < PER_SET)
    spread = one_hot(same & (across == row // ROWS)).astype(BF16)
    spread_ref[...] = spread
    out_ref[...] = dot(spread, pieces_ref[...]).astype(BF16)


def select_kernel(select_ref, pieces_ref, out_ref):
    out_ref[...] = dot(select_ref[...], pieces_ref[...]).astype(BF16)


def sum_of(pieces_ref):
    total = pieces_ref[0].astype(F32)
    for m in range(1, pieces_ref.shape[0]):
        total = total + pieces_ref[m].astype(F32)
    return total


def copies(out_ref, value):
    for m in range(out_ref.shape[0]):
        out_ref[m] = value


def first_rhs_kernel(pieces_ref, out_ref):
    copies(out_ref, (-sum_of(pieces_ref)).astype(BF16))


def rhs_kernel(where_ref, pieces_ref, step_ref, scale_ref, out_ref):
    step = step_ref[where_ref[1]].astype(F32)
    side = -scale_ref[pl.ds(where_ref[0], 1), :] * step
    copies(out_ref, (side - sum_of(pieces_ref)).astype(BF16))


def fetched_step_kernel(pieces_ref, inverse_hbm, out_ref, inverse_ref, sems):
    fetches = [
        pltpu.make_async_copy(inverse_hbm.at[zh], inverse_ref.at[zh], sems.at[zh])
        for zh in range(2)
    ]
    for fetch in fetches:
        fetch.start()
    step_kernel(pieces_ref, inverse_ref, out_ref, fetches)


def step_kernel(pieces_ref, inverse_ref, out_ref, fetches=()):
    rhs = jnp.concatenate([pieces_ref[m] for m in range(pieces_ref.shape[0])], axis=1)
    parts = []
    for zh in range(2):
        if fetches:
            fetches[zh].wait()
        parts.append(dot(rhs, inverse_ref[zh]))
    parts = [part[:, h * PANEL : (h + 1) * PANEL] for part in parts for h in range(2)]
    copies(out_ref, jnp.concatenate(parts, axis=0).astype(BF16))


def total_kernel(pieces_ref, out_ref):
    copies(out_ref, sum_of(pieces_ref).astype(BF16))


def last_total_kernel(pieces_ref, out_ref, own_ref):
    total = sum_of(pieces_ref).astype(BF16)
    copies(out_ref, total)
    own_ref[...] = total


def last_pick_kernel(select_ref, pieces_ref, own_ref, *refs):
    out_ref, size = refs[-1], PB * ROWS
    picked = [ref[...] for ref in refs[:-1]]
    picked.append(dot(select_ref[...], pieces_ref[...]).astype(BF16))
    for zi in range(SETS):
        half = (zi // 4) * 2 * ROWS
        for k, rows in enumerate(picked):
            out_ref[zi, k * size : (k + 1) * size] = rows[zi * size : (zi + 1) * size]
        out_ref[zi, len(picked) * size :] = own_ref[half : half + 2 * ROWS]


def correct(rhs_ref, scale_ref, leaf):
    return (rhs_ref[...].astype(F32) - scale_ref[...] * leaf.astype(F32)).astype(BF16)


def in_chunks(body, rows, chunk=256):
    def step(i, carry):
        body(pl.ds(pl.multiple_of(i * chunk, chunk), chunk))
        return carry

    lax.fori_loop(0, rows // chunk, step, 0)


def first_response_kernel(after_ref, scale_ref, tile_ref, coupling_ref, out_ref, solved_ref):
    def some(rows):
        leaf = by_tiles(tile_ref, coupling_ref[rows, :])
        solved = by_tiles(tile_ref, (scale_ref[...] * leaf.astype(F32)).astype(BF16))
        solved_ref[rows, :] = solved
        out_ref[rows, :] = dot_t(solved, coupling_ref[...]).astype(BF16)

    in_chunks(some, out_ref.shape[0])


def response_kernel(after_ref, earlier_ref, scale_ref, tile_ref, coupling_ref, out_ref, solved_ref):
    def some(rows):
        moved = (-scale_ref[...] * earlier_ref[rows, :].astype(F32)).astype(BF16)
        solved = by_tiles(tile_ref, moved)
        solved_ref[rows, :] = solved
        out_ref[rows, :] = dot_t(solved, coupling_ref[...]).astype(BF16)

    in_chunks(some, out_ref.shape[0])


def ahead_kernel(
    pieces_ref, unpack_ref, pack_ref, rhs_ref, scale_ref, tile_ref, coupling_ref,
    out_ref, next_ref, state_ref,
):
    size = PB * ROWS
    rows = dot(unpack_ref[...], pieces_ref[...]).astype(BF16)
    leaf = solve_leaf(rows, rhs_ref[...], tile_ref, coupling_ref)
    corrected = correct(rhs_ref, scale_ref, leaf)
    next_ref[...] = corrected
    state_ref[...] = corrected

    def solve(k, carry):
        solved = by_tiles(tile_ref, state_ref[...])
        state_ref[...] = correct(rhs_ref, scale_ref, solved)
        pieces = touched_pieces(solved, coupling_ref, pack_ref[...]).astype(BF16)
        rows = pl.ds(pl.multiple_of(k * size, size), size)
        for zi in range(SETS):
            out_ref[zi, rows, :] = pieces[zi * size : (zi + 1) * size]
        return carry

    lax.fori_loop(0, SOLVES - 1, solve, 0, unroll=True)


def ahead_rows(ahead_ref, k):
    size = PB * ROWS
    return jnp.concatenate(
        [ahead_ref[zi, (k - 1) * size : k * size] for zi in range(SETS)], axis=0
    )


def ahead_spread_kernel(spread_ref, ahead_ref, out_ref):
    out_ref[...] = dot(spread_ref[...], ahead_rows(ahead_ref, 1)).astype(BF16)


def fetch_all(response_hbm, response_ref, sems):
    fetches = [
        pltpu.make_async_copy(response_hbm.at[zi], response_ref.at[zi], sems.at[zi])
        for zi in range(SETS)
    ]
    for fetch in fetches:
        fetch.start()
    return fetches


def responses(fetches, picked_ref, response_ref):
    rows = []
    for zi in range(SETS):
        starts = [(zi * PB + s) * ROWS for s in range(PB)]
        picked = jnp.concatenate([picked_ref[r : r + ROWS] for r in starts], axis=1)
        fetches[zi].wait()
        added = dot(picked, response_ref[zi])
        rows += [added[:, s * PANEL : (s + 1) * PANEL] for s in range(PB)]
    return jnp.concatenate(rows, axis=0)


def respond_kernel(base_ref, picked_ref, spread_ref, response_hbm, out_ref, response_ref, sems):
    fetches = fetch_all(response_hbm, response_ref, sems)
    base = ahead_rows(base_ref, 2) if base_ref.ndim == 3 else base_ref[...]
    touched = base.astype(F32) + responses(fetches, picked_ref, response_ref)
    out_ref[...] = dot(spread_ref[...], touched.astype(BF16)).astype(BF16)


def third_base_kernel(ahead_ref, picked_ref, response_hbm, out_ref, response_ref, sems):
    fetches = fetch_all(response_hbm, response_ref, sems)
    added = responses(fetches, picked_ref, response_ref)
    out_ref[...] = ahead_rows(ahead_ref, 3).astype(F32) + added


def fourth_base_kernel(
    ahead_ref, near_ref, far_ref, near_hbm, far_hbm, out_ref,
    near_response_ref, far_response_ref, near_sems, far_sems,
):
    near = fetch_all(near_hbm, near_response_ref, near_sems)
    far = fetch_all(far_hbm, far_response_ref, far_sems)
    added = responses(near, near_ref, near_response_ref)
    added = added + responses(far, far_ref, far_response_ref)
    out_ref[...] = ahead_rows(ahead_ref, 4).astype(F32) + added


def last_kernel(
    pieces_ref, unpack_ref, corrected_ref, rhs_ref, scale_ref, tile_ref, coupling_ref,
    leaf_ref, link_ref, state_ref,
):
    columns, size = corrected_ref.shape[0], PB * ROWS
    state_ref[...] = corrected_ref[...]

    def solve(k, carry):
        at = pl.ds(pl.multiple_of(k * size, size), size)
        pieces = jnp.concatenate([pieces_ref[zi, at, :] for zi in range(SETS)], axis=0)
        rows = dot(unpack_ref[...], pieces).astype(BF16)
        leaf = solve_leaf(rows, state_ref[...], tile_ref, coupling_ref)
        leaf_ref[...] = leaf
        state_ref[...] = correct(rhs_ref, scale_ref, leaf)
        return carry

    lax.fori_loop(0, SOLVES - 1, solve, 0)
    link = jnp.concatenate([pieces_ref[zi, (SOLVES - 1) * size :] for zi in range(SETS)], axis=0)
    link = dot(unpacker(2), link).astype(BF16)
    link_ref[...] = jnp.concatenate([link[:columns], link[columns:]], axis=1)


INTERPRET = False


def call(body, shapes, *operands, fetched=(), queues=1, state=(), dtype=BF16):
    outs = [jax.ShapeDtypeStruct(s, dtype) for s in shapes]
    vmem, smem, anywhere = (
        pl.BlockSpec(memory_space=s) for s in (pltpu.VMEM, pltpu.SMEM, pltpu.HBM)
    )
    operands = [
        pltpu.with_memory_space_constraint(x, pltpu.HBM) if i in fetched and not INTERPRET else x
        for i, x in enumerate(operands)
    ]
    scratch = [pltpu.VMEM(s, BF16) for s in state]
    scratch += [pltpu.VMEM(operands[i].shape, BF16) for i in fetched]
    if fetched:
        scratch += [pltpu.SemaphoreType.DMA((SETS,))] * queues
    return pl.pallas_call(
        body,
        out_shape=outs,
        in_specs=[
            anywhere if i in fetched else smem if x.dtype == I32 else vmem
            for i, x in enumerate(operands)
        ],
        out_specs=[vmem] * len(outs),
        scratch_shapes=scratch,
        compiler_params=pltpu.CompilerParams(vmem_limit_bytes=24 << 20),
        interpret=INTERPRET,
    )(*operands)


def swap(x, axes):
    return lax.all_to_all(x, axes, 0, 0, tiled=True)


def per_device(
    tile_inverse, link_coupling, link_panels, leaf_rhs, leaf_scale, link_scale, link_inverse
):
    tile_inv, coupling, own_rhs = tile_inverse[0], link_coupling[0], leaf_rhs[0]
    columns = own_rhs.shape[0]
    assert columns == SETS * PER_SET
    x, y, core = lax.axis_index("x"), lax.axis_index("y"), lax.axis_index("core")
    line, members = lax.axis_size(LINE), lax.axis_size(GROUP)

    inverse = lax.all_gather(link_inverse, Z)
    inverse = inverse.reshape(2, -1, link_inverse.shape[1])
    scales = link_scale.reshape(-1, PANEL)
    place = y * 2 + core
    panel = (place >> 2) * 16 + x * 4 + (place & 3)
    where = jnp.stack([panel, place_of(panel)]).astype(I32)

    home = (SETS * PB * ROWS, PANEL)
    flat = (members * ROWS, PANEL)
    mixer = (PB * columns, SETS * PB * ROWS)
    parts = (4 * ROWS, PANEL)
    pieces, pack, unpack = call(
        first_kernel, [home, mixer[::-1], mixer], link_panels, own_rhs, tile_inv, coupling,
        fetched=(1, 2, 3),
    )
    sent = (SETS, PB * ROWS, PANEL)
    blocks = (leaf_scale, tile_inv, coupling)
    answers, picks = [], []
    for k in range(SOLVES):
        last = k == SOLVES - 1
        if k == 0:
            pieces, spread, pick = call(
                first_spread_kernel, [flat, (flat[0], home[0]), (home[0], flat[0])],
                swap(pieces.reshape(sent), Z).reshape(home),
            )
        elif k == 1:
            pieces, = call(ahead_spread_kernel, [flat], spread, ahead)
        else:
            base = ahead if k == 2 else base
            pieces, = call(
                respond_kernel, [flat], base, picks[-1], spread, answers[0], fetched=(3,)
            )
        if k < 3:
            answer = [(PB * PANEL,) * 2, (PB * PANEL, own_rhs.shape[1])]
            if k == 0:
                answer, solved = call(first_response_kernel, answer, pieces, *blocks)
            else:
                answer, solved = call(response_kernel, answer, pieces, solved, *blocks)
            answers.append(lax.all_gather(answer, Z))
        pieces = swap(pieces.reshape(members, ROWS, PANEL), GROUP)
        if k == 0:
            pieces, = call(first_rhs_kernel, [(line, ROWS, PANEL)], pieces)
        else:
            pieces, = call(rhs_kernel, [(line, ROWS, PANEL)], where, pieces, step, scales)
        pieces = swap(pieces, LINE)
        if k < 3:
            pieces, = call(fetched_step_kernel, [(4,) + parts], pieces, inverse, fetched=(1,))
        else:
            pieces, = call(step_kernel, [(4,) + parts], pieces, inverse)
        pieces = swap(pieces, "x")
        if last:
            pieces, own = call(last_total_kernel, [(line,) + parts, parts], pieces)
        else:
            pieces, = call(total_kernel, [(line,) + parts], pieces)
        pieces = swap(pieces, LINE)
        if k == 2:
            base, = call(
                third_base_kernel, [home], ahead, picks[0], answers[1],
                fetched=(2,), dtype=F32,
            )
        elif k == 3:
            base, = call(
                fourth_base_kernel, [home],
                ahead, picks[1], picks[0], answers[1], answers[2],
                fetched=(3, 4), queues=2, dtype=F32,
            )
        step, pieces = pieces.reshape(members, ROWS, PANEL), pieces.reshape(flat)
        if last:
            wide = (SETS, ((SOLVES - 1) * PB + 2) * ROWS, PANEL)
            pieces, = call(last_pick_kernel, [wide], pick, pieces, own, *picks)
            leaf, link = call(
                last_kernel, [own_rhs.shape, (columns, 2 * PANEL)],
                swap(pieces, Z), unpack, corrected, own_rhs, *blocks, state=(own_rhs.shape,),
            )
        else:
            picked, = call(select_kernel, [home], pick, pieces)
            if k == 0:
                ahead, corrected = call(
                    ahead_kernel, [(SETS, (SOLVES - 1) * PB * ROWS, PANEL), own_rhs.shape],
                    swap(picked.reshape(sent), Z).reshape(home),
                    unpack, pack, own_rhs, *blocks, state=(own_rhs.shape,),
                )
                ahead = swap(ahead, Z)
            else:
                picks.append(picked)
    return leaf[None], link


def solution(mesh):
    fine = Mesh(mesh.devices.reshape(4, 4, 8, 2, 2), SPLIT)
    sec, dev = SPLIT[:2], SPLIT[2:]
    in_specs = (
        P(SPLIT, None, None, None),
        P(SPLIT, None, None),
        P(SPLIT, None),
        P(SPLIT, None, None),
        P(SPLIT, None),
        P(),
        P(sec, dev),
    )
    out_specs = (P(SPLIT, None, None), P(None, dev))
    return jax.shard_map(
        per_device, mesh=fine, in_specs=in_specs, out_specs=out_specs, check_vma=False
    )
```
